512 devices in a mesh: rows: 16 (over x, y_hi, core), cols: 32 (over y_lo, z).
Axes of the slice: x: 4, y: 8 (y_hi: 2, y_lo: 4; y = y_hi * 4 + y_lo), z: 8, core: 2. Of those that a mesh axis runs over, the one named last changes fastest.
Arguments:
- field: bfloat16 [32, 64, 32768], P('cols', 'rows'), may hold values from -6 to 6
- depth_kernel: float32 [7, 7, 32], replicated, may hold values from -0.875 to 0.875
- point_weight: bfloat16 [32, 32], replicated, may hold values from -1 to 1
- point_bias: float32 [32], replicated, may hold values from -3 to 3
- vert_weight: bfloat16 [2, 288, 32], replicated, may hold values from -0.375 to 0.375
- vert_bias: float32 [2, 32], replicated, may hold values from -3 to 3
- exhaust: bfloat16 [262144, 32], P(('rows', 'cols')), may hold values from -6 to 6
- owner: int32 [262144, 1], P(('rows', 'cols')), may hold values from 0 to 31; in each aligned block of 512 rows (0 to 511, 512 to 1023, ...) at most 32 rows name the same one
- cells: int32 [262144], P(('rows', 'cols')), may hold values from 0 to 4095
Outputs:
- advanced: bfloat16 [32, 64, 32768], P(None, 'rows', 'cols')
The draws below stay inside these ranges and needn't reach their ends.
Inputs may be any that keep to these rules, and one draw needn't show every extreme that they name: `owner`: among the 512 rows of one device, no tile is named by more than 32 rows, a bound that some block reaches.
All inputs are finite; a program needn't handle non-finite values.
Results may differ from the reference program's by a relative error of at most 0.0055.
Values may be sent and summed in bfloat16 or wider, within the bound.
A program may use at most 128 MiB of HBM per device.

```python
import math
import jax
import jax.numpy as jnp
import numpy as np
from jax import lax

C = 32
X = 1024
Z = 32
YB = 4
E_DEV = 512
KH = 7
KV = 9
LAYERS = 2
Y = 64
XT = 32
CAP = 32
EXH = 262144
N_ROWS = 16
N_COLS = 32


def plant(values, own_key, low, top_value):
    place = [jax.random.randint(jax.random.fold_in(own_key, axis), (), 0, length) for axis, length in enumerate(values.shape)]
    widest = values.shape.index(max(values.shape))
    beside = place[:widest] + [(place[widest] + 1) % values.shape[widest]] + place[widest + 1:]
    return values.at[tuple(place)].set(low).at[tuple(beside)].set(top_value)


def block_scale(rng, dims, shards, low, top_value):
    def one(dim, parts):
        heights = jax.random.uniform(jax.random.fold_in(jax.random.fold_in(rng, 6), dim), (parts,), jnp.float32, low / len(shards), top_value / len(shards))
        return jnp.repeat(jnp.exp(heights), dims[dim] // parts).reshape((-1,) + (1,) * (len(dims) - dim - 1))

    gain = one(*shards[0])
    for cut in shards[1:]:
        gain = gain * one(*cut)
    return gain


def routed_block(rng, own, number, rows, amount, top, most, skew):
    ranking = jax.random.permutation(rng, amount)
    packed, ordinary = portions_of(amount, rows * top, most, skew, True), portions_of(amount, rows * top, most, skew, False)
    places = jnp.arange(amount)

    def named(tallies, rotation):
        used = int((tallies > 0).sum())
        fixed = max(1, used // 4)
        moved = fixed + (places - fixed + rotation * (used - fixed)) % max(1, amount - fixed)
        return jnp.zeros((amount,), jnp.int32).at[ranking[jnp.where(places < fixed, places, moved)]].set(jnp.asarray(tallies, jnp.int32))

    tallies = jnp.where(number % 4 == 0, named(packed, number // 4), named(ordinary, number - number // 4 - 1))
    mixed = jax.random.permutation(jax.random.fold_in(own, 3), amount)
    source_of, taker = mixed[0:amount // 2 * 2:2], mixed[1:amount // 2 * 2:2]
    room = jnp.minimum(tallies[source_of] - 1, most - tallies[taker]) // 2
    room = jnp.where((source_of == ranking[0]) | (taker == ranking[0]) | (tallies[taker] == 0), 0, jnp.maximum(room, 0))
    moved = jax.random.randint(jax.random.fold_in(own, 4), (amount // 2,), 0, 1 << 20) % (room + 1)
    tallies = tallies.at[source_of].add(-moved).at[taker].add(moved)
    items = jnp.searchsorted(jnp.cumsum(tallies), jnp.arange(rows * top), side="right").astype(jnp.int32)
    table = items.reshape(top, rows).T
    table = table[jax.random.permutation(jax.random.fold_in(own, 1), rows)]
    rotation = jax.random.randint(jax.random.fold_in(own, 2), (rows, 1), 0, top)
    return jnp.take_along_axis(table, (jnp.arange(top)[None, :] + rotation) % top, axis=1)


def portions_of(amount, total, limit, lean, full):
    weights = [(1 << 20) // math.isqrt(standing ** lean) + 1 for standing in range(1, amount + 1)]
    largest = limit if full else min(limit, max(-(-total // amount), total * weights[0] // sum(weights)))
    least = 1 if total - largest >= amount - 1 else 0
    counts, rest = [largest] + [least] * (amount - 1), total - largest - least * (amount - 1)
    while rest > 0:
        movable = [i for i in range(1, amount) if counts[i] < largest] or [i for i in range(1, amount) if counts[i] < limit]
        pool, remaining = sum([weights[i] for i in movable]), rest
        for i in movable:
            extra = min(limit - counts[i], max(1, remaining * weights[i] // pool), rest)
            counts[i] = counts[i] + extra
            rest = rest - extra
    return np.array(counts)


def centred(rng, dims, scale, limit, shards=(), kind=jnp.bfloat16):
    factor_of = block_scale(rng, dims, shards, -0.22, 0.18) if shards else 1.0
    array = jax.random.normal(rng, dims, jnp.float32) * scale * factor_of
    return jnp.minimum(jnp.maximum(array, -limit), limit).astype(kind)


def setup_inputs(seed: int = 0) -> dict:
    splits = jax.random.split(jax.random.key(seed), 10)
    field = centred(splits[0], (Z, Y, X * C), 1.0, 6.0, ((0, 32), (1, 16)))
    depth_kernel = centred(splits[1], (KH, KH, C), (KH * KH) ** -0.5, 0.875, (), jnp.float32)
    point_weight = centred(splits[2], (C, C), C ** -0.5, 1.0)
    point_bias = centred(splits[3], (C,), 0.5, 3.0, (), jnp.float32)
    vert_weight = centred(splits[4], (LAYERS, KV * C, C), (KV * C) ** -0.5, 0.375)
    vert_bias = centred(splits[5], (LAYERS, C), 0.5, 3.0, (), jnp.float32)
    exhaust = centred(splits[6], (EXH, C), 1.0, 6.0, ((0, 512),))
    owner_keys = jax.random.split(jax.random.fold_in(splits[7], 1), EXH // E_DEV)
    owner_turns = jax.random.permutation(jax.random.fold_in(splits[7], 3), EXH // E_DEV)
    owner = jax.vmap(lambda own, number: routed_block(jax.random.fold_in(splits[7], 2), own, number, E_DEV, N_COLS, 1, CAP, 2))(owner_keys, owner_turns).reshape((EXH, 1))
    cells = plant(jax.random.randint(splits[8], (EXH,), 0, Z * YB * (X // N_COLS)), jax.random.fold_in(splits[8], 1), 0, (Z * YB * (X // N_COLS)) - 1).astype(jnp.int32)
    return {"field": field, "depth_kernel": depth_kernel, "point_weight": point_weight, "point_bias": point_bias, "vert_weight": vert_weight, "vert_bias": vert_bias, "exhaust": exhaust, "owner": owner, "cells": cells}


def horizontal(band, depth_kernel, point_weight, point_bias):
    height = band.shape[1] - 6
    width = band.shape[2] - 6
    total = jnp.zeros((band.shape[0], height, width, C), jnp.float32)
    for i in range(KH):
        for j in range(KH):
            total = total + band[:, i:i + height, j:j + width, :].astype(jnp.float32) * depth_kernel[i, j]
    depth_b = total.astype(jnp.bfloat16)
    proj = jnp.einsum("zyxc,cd->zyxd", depth_b.astype(jnp.float32), point_weight.astype(jnp.float32))
    center = band[:, 3:3 + height, 3:3 + width, :].astype(jnp.float32)
    return (center + jax.nn.gelu(proj + point_bias)).astype(jnp.bfloat16)


def vertical(level_field, vert_weight, vert_bias):
    current = level_field
    result = None
    for layer in range(LAYERS):
        padded = jnp.pad(current, ((4, 4), (0, 0), (0, 0), (0, 0)))
        conv = jnp.zeros(current.shape, jnp.float32) + vert_bias[layer]
        for k in range(KV):
            conv = conv + jnp.einsum("zyxc,cd->zyxd", padded[k:k + Z].astype(jnp.float32),
                                     vert_weight[layer, k * C:(k + 1) * C].astype(jnp.float32))
        result = current.astype(jnp.float32) + jax.nn.gelu(conv)
        if layer < LAYERS - 1:
            current = result.astype(jnp.bfloat16)
    return result


def reference(field, depth_kernel, point_weight, point_bias, vert_weight, vert_bias, exhaust, owner, cells):
    padded = jnp.pad(field, ((0, 0), (3, 3), (0, 0)))
    band_rows = N_COLS * E_DEV

    def one_band(band_index):
        start = (band_index * YB).astype(jnp.int32)
        band = lax.dynamic_slice_in_dim(padded, start, YB + 6, 1).reshape(Z, YB + 6, X, C)
        band = jnp.pad(band, ((0, 0), (0, 0), (3, 3), (0, 0)))
        mixed = horizontal(band, depth_kernel, point_weight, point_bias)
        pre = vertical(mixed, vert_weight, vert_bias)
        first = (band_index * band_rows).astype(jnp.int32)
        emis = lax.dynamic_slice_in_dim(exhaust, first, band_rows, 0).astype(jnp.float32)
        where_to = lax.dynamic_slice_in_dim(owner, first, band_rows, 0)[:, 0]
        which = lax.dynamic_slice_in_dim(cells, first, band_rows, 0)
        level = which // (YB * XT)
        yrow = (which // XT) % YB
        xcol = where_to * XT + which % XT
        source = jnp.zeros((Z, YB, X, C), jnp.float32).at[level, yrow, xcol].add(emis)
        return (pre + source).astype(jnp.bfloat16).reshape(Z, YB, X * C)

    bands = lax.map(one_band, jnp.arange(N_ROWS, dtype=jnp.int32))
    return jnp.transpose(bands, (1, 0, 2, 3)).reshape(Z, Y, X * C)
```

```python
import jax
import jax.numpy as jnp
from jax import lax
from jax.experimental import pallas as pl
from jax.experimental.pallas import tpu as pltpu
from jax.sharding import PartitionSpec as P

C = 32
X = 1024
Z = 32
YB = 4
KH = 7
KV = 9
LAYERS = 2
E_DEV = 512
N_ROWS = 16
N_COLS = 32
LANES = 128
TILES = X * C // LANES
MSG = YB * TILES // N_COLS
MESH = pl.DeviceIdType.MESH
BF = jnp.bfloat16
F32 = jnp.float32
HIGH = lax.Precision.HIGHEST


def iota(shape, dim):
    return lax.broadcasted_iota(jnp.int32, shape, dim)


def dot(a, b):
    return jnp.dot(a, b, preferred_element_type=F32)


def select_matrix(rows, lanes):
    return iota((rows, lanes), 0) == iota((rows, lanes), 1) % rows


def lane_tile(x, lanes):
    return jnp.dot(
        x, select_matrix(C, lanes).astype(F32), preferred_element_type=F32, precision=HIGH
    )


def pack_exhaust(me, ex_ref, own_ref, cell_ref, xs):
    owner = own_ref[...]
    cell = cell_ref[...]
    onehot = iota((N_COLS, E_DEV), 0) == owner
    before = (iota((E_DEV, E_DEV), 0) < iota((E_DEV, E_DEV), 1)).astype(F32).astype(BF)
    earlier = dot(onehot.astype(F32).astype(BF), before)
    rank = jnp.sum(jnp.where(onehot, earlier, 0.0), axis=0, keepdims=True)
    rank_i = rank.astype(jnp.int32)
    level = cell >> 7
    y = (cell >> 5) & 3
    x = cell & 31
    low = ((x >> 2) << 2) + y
    zero = jnp.zeros((1, E_DEV), F32)
    values = jnp.concatenate(
        [level.astype(F32), low.astype(F32), (x & 3).astype(F32), rank, zero, zero, zero, zero],
        axis=0,
    )
    rank_col = jnp.transpose(values)[:, 3:4].astype(jnp.int32)
    lane = iota((E_DEV, LANES), 1)
    tiled = dot(ex_ref[...], select_matrix(C, LANES).astype(F32).astype(BF))
    placed = jnp.where(lane // C == rank_col // 8, tiled, 0.0).astype(BF)
    row = iota((N_COLS * 8, E_DEV), 0)
    to_row = (row == owner * 8 + rank_i % 8).astype(F32).astype(BF)
    data = dot(to_row, placed)
    spread = jnp.broadcast_to(values[None], (N_COLS, 8, E_DEV)).reshape(N_COLS * 8, E_DEV)
    meta_rows = jnp.where(row // 8 == owner, spread, 0.0).astype(BF)
    meta_lane = (lane == rank_col + (me % 4) * 32).astype(F32).astype(BF)
    meta = dot(meta_rows, meta_lane)
    xs[...] = jnp.concatenate(
        [data.reshape(N_COLS, 8, LANES), meta.reshape(N_COLS, 8, LANES)], axis=1
    ).astype(BF)


def add_exhaust(xr, codes, rows_b, source):
    got = xr[...].astype(F32)
    data = got[:, :8, :].reshape(N_COLS * 8, LANES).astype(BF)
    m = iota((LANES, 4 * LANES), 0)
    n = iota((LANES, 4 * LANES), 1)
    expand = ((m // C == n // LANES) & (m % C == n % C)).astype(F32).astype(BF)
    wide = dot(data, expand)
    by_slot = jnp.concatenate(
        [wide[:, g * LANES : (g + 1) * LANES].reshape(N_COLS, 1, 8, LANES) for g in range(4)],
        axis=1,
    ).reshape(N_COLS * 32, LANES)
    lane = iota((LANES, LANES), 1)
    for b in range(8):
        meta = got[4 * b, 8:, :]
        for k in range(1, 4):
            meta = meta + got[4 * b + k, 8:, :]
        codes[:, b * LANES : (b + 1) * LANES] = meta[0:1] * 32.0 + meta[1:2]
        place = jnp.transpose(meta)[:, 2:3].astype(jnp.int32)
        rows_b[b * LANES : (b + 1) * LANES, :] = jnp.where(
            lane // C == place, by_slot[b * LANES : (b + 1) * LANES, :], 0.0
        ).astype(BF)

    @pl.loop(0, 4)
    def _(block):
        base = pl.multiple_of(block * 256, 256)
        row = (iota((256, N_COLS * 32), 0) + base).astype(F32)
        hit = (row == codes[...]).astype(F32).astype(BF)
        source[pl.ds(base, 256), :] = dot(hit, rows_b[...])


def horizontal_weights(dk_ref, pw_ref, dk_pad, hw):
    for i in range(KH):
        dk_pad[i * 8 : i * 8 + KH, 0:C] = dk_ref[i]
    columns = jnp.transpose(dk_pad[...])[0:C, :]
    point = dot(pw_ref[...], select_matrix(C, 2 * LANES).astype(F32).astype(BF))
    block = iota((C, 2 * LANES), 1) // C
    for i in range(KH):
        taps = jnp.zeros((C, 2 * LANES), F32)
        for m in range(KH):
            j = KH - 1 - m
            taps = jnp.where(block == m, columns[:, i * 8 + j : i * 8 + j + 1], taps)
        taps = jnp.concatenate([taps * point, jnp.zeros((C, LANES), F32)], axis=1)
        for cell in range(4):
            start = i * LANES + cell * C
            hw[start : start + C, :] = pltpu.roll(taps, (cell + 1) * C, 1).astype(BF)


def vertical_weights(vw_ref, vw):
    row = iota((LANES, LANES), 0)
    lane = iota((LANES, LANES), 1)
    for layer in range(LAYERS):
        wide = dot(vw_ref[layer], select_matrix(C, LANES).astype(F32).astype(BF))
        for k in range(KV):
            part = wide[k * C : (k + 1) * C, :]
            whole = jnp.concatenate([part, part, part, part], axis=0)
            vw[layer, k * LANES : (k + 1) * LANES, :] = jnp.where(
                row // C == lane // C, whole, 0.0
            ).astype(BF)


def kernel(
    field_ref, dk_ref, pw_ref, pb_ref, vw_ref, vb_ref, ex_ref, own_ref, cell_ref, out_ref,
    stage, band, dk_pad, hw, vw, send, recv, mid, xs, xr, codes, rows_b, source,
    halo_send, halo_recv, mix_send, mix_recv, ex_send, ex_recv,
):
    r = lax.axis_index("rows")
    me = lax.axis_index("cols")
    barrier = pltpu.get_barrier_semaphore()

    @pl.loop(1, N_COLS)
    def _(s):
        pl.semaphore_signal(
            barrier, inc=1, device_id={"cols": lax.rem(me + s, N_COLS)}, device_id_type=MESH
        )

    for step in (1, N_ROWS - 1):
        pl.semaphore_signal(
            barrier, inc=1, device_id={"rows": lax.rem(r + step, N_ROWS)}, device_id_type=MESH
        )

    stage[...] = field_ref[...].astype(F32)
    for y in range(YB):
        band[3 + y] = stage[pl.ds(y, TILES, stride=YB), :].astype(BF)

    @pl.when(r == 0)
    def _():
        band[0:3] = jnp.zeros((3, TILES, LANES), BF)

    @pl.when(r == N_ROWS - 1)
    def _():
        band[7:10] = jnp.zeros((3, TILES, LANES), BF)

    pl.semaphore_wait(barrier, N_COLS + 1)

    to_next = pltpu.make_async_remote_copy(
        src_ref=band.at[4:7], dst_ref=band.at[0:3], send_sem=halo_send.at[0],
        recv_sem=halo_recv.at[0], device_id={"rows": lax.rem(r + 1, N_ROWS)},
        device_id_type=MESH,
    )
    to_last = pltpu.make_async_remote_copy(
        src_ref=band.at[3:6], dst_ref=band.at[7:10], send_sem=halo_send.at[1],
        recv_sem=halo_recv.at[1], device_id={"rows": lax.rem(r + N_ROWS - 1, N_ROWS)},
        device_id_type=MESH,
    )

    @pl.when(r < N_ROWS - 1)
    def _():
        to_next.start()

    @pl.when(r > 0)
    def _():
        to_last.start()

    pack_exhaust(me, ex_ref, own_ref, cell_ref, xs)

    def exhaust_copy(s):
        there = lax.rem(me + s, N_COLS)
        return pltpu.make_async_remote_copy(
            src_ref=xs.at[there], dst_ref=xr.at[me], send_sem=ex_send.at[there],
            recv_sem=ex_recv.at[me], device_id={"cols": there}, device_id_type=MESH,
        )

    def exhaust_arrival(s):
        there = lax.rem(me + s, N_COLS)
        return pltpu.make_async_remote_copy(
            src_ref=xs.at[there], dst_ref=xr.at[there], send_sem=ex_send.at[there],
            recv_sem=ex_recv.at[there], device_id={"cols": there}, device_id_type=MESH,
        )

    def mixed_copy(s):
        there = lax.rem(me + s, N_COLS)
        return pltpu.make_async_remote_copy(
            src_ref=send.at[there], dst_ref=recv.at[4 + me], send_sem=mix_send.at[there],
            recv_sem=mix_recv.at[me], device_id={"cols": there}, device_id_type=MESH,
        )

    def mixed_arrival(s):
        there = lax.rem(me + s, N_COLS)
        return pltpu.make_async_remote_copy(
            src_ref=send.at[there], dst_ref=recv.at[4 + there], send_sem=mix_send.at[there],
            recv_sem=mix_recv.at[there], device_id={"cols": there}, device_id_type=MESH,
        )

    @pl.loop(1, N_COLS)
    def _(s):
        exhaust_copy(s).start()

    xr[me] = xs[me]
    horizontal_weights(dk_ref, pw_ref, dk_pad, hw)
    vertical_weights(vw_ref, vw)
    bias_h = lane_tile(pb_ref[...], LANES)
    bias_v = lane_tile(vb_ref[...], LANES)
    edge = jnp.zeros((4, MSG, LANES), BF)
    for buffer in (recv, mid):
        buffer[0:4] = edge
        buffer[4 + Z : 8 + Z] = edge

    @pl.when(r > 0)
    def _():
        to_next.wait_recv()

    @pl.when(r < N_ROWS - 1)
    def _():
        to_last.wait_recv()

    row = iota((TILES, LANES), 0)
    for y in range(YB):
        rows = jnp.concatenate([band[y + i] for i in range(KH)], axis=1)
        parts = dot(rows, hw[...])
        right = pltpu.roll(parts[:, 0:LANES], TILES - 1, 0)
        left = pltpu.roll(parts[:, 2 * LANES : 3 * LANES], 1, 0)
        total = (
            parts[:, LANES : 2 * LANES]
            + jnp.where(row < TILES - 1, right, 0.0)
            + jnp.where(row > 0, left, 0.0)
        )
        stage[pl.ds(y, TILES, stride=YB), :] = band[3 + y].astype(F32) + jax.nn.gelu(
            total + bias_h
        )
    send[...] = stage[...].astype(BF).reshape(N_COLS, MSG, LANES)

    @pl.loop(1, N_COLS)
    def _(s):
        mixed_copy(s).start()

    recv[4 + me] = send[me]

    @pl.loop(1, N_COLS)
    def _(s):
        exhaust_arrival(s).wait_recv()

    add_exhaust(xr, codes, rows_b, source)

    @pl.loop(1, N_COLS)
    def _(s):
        mixed_arrival(s).wait_recv()

    def conv(buffer, layer, block):
        rows = jnp.concatenate(
            [buffer[pl.ds(block * 8 + k, 8)].reshape(8 * MSG, LANES) for k in range(KV)], axis=1
        )
        before = buffer[pl.ds(block * 8 + 4, 8)].reshape(8 * MSG, LANES).astype(F32)
        return before + jax.nn.gelu(dot(rows, vw[layer]) + bias_v[layer : layer + 1])

    @pl.loop(0, 4)
    def _(block):
        mid[pl.ds(block * 8 + 4, 8)] = conv(recv, 0, block).astype(BF).reshape(8, MSG, LANES)

    @pl.loop(0, 4)
    def _(block):
        base = pl.multiple_of(block * 256, 256)
        result = conv(mid, 1, block) + source[pl.ds(base, 256), :]
        out_ref[pl.ds(base, 256), :] = result.astype(BF)

    @pl.when(r < N_ROWS - 1)
    def _():
        to_next.wait_send()

    @pl.when(r > 0)
    def _():
        to_last.wait_send()

    @pl.loop(1, N_COLS)
    def _(s):
        exhaust_copy(s).wait_send()
        mixed_copy(s).wait_send()


def body(
    field, depth_kernel, point_weight, point_bias, vert_weight, vert_bias, exhaust, owner, cells
):
    rows = field.reshape(YB, TILES, LANES).transpose(1, 0, 2).reshape(TILES * YB, LANES)
    out = pl.pallas_call(
        kernel,
        out_shape=jax.ShapeDtypeStruct((Z * MSG, LANES), BF),
        in_specs=[pl.BlockSpec(memory_space=pltpu.VMEM)] * 9,
        out_specs=pl.BlockSpec(memory_space=pltpu.VMEM),
        scratch_shapes=[
            pltpu.VMEM((TILES * YB, LANES), F32),
            pltpu.VMEM((YB + 6, TILES, LANES), BF),
            pltpu.VMEM((LANES, LANES), F32),
            pltpu.VMEM((KH * LANES, 3 * LANES), BF),
            pltpu.VMEM((LAYERS, KV * LANES, LANES), BF),
            pltpu.VMEM((N_COLS, MSG, LANES), BF),
            pltpu.VMEM((Z + 8, MSG, LANES), BF),
            pltpu.VMEM((Z + 8, MSG, LANES), BF),
            pltpu.VMEM((N_COLS, 16, LANES), BF),
            pltpu.VMEM((N_COLS, 16, LANES), BF),
            pltpu.VMEM((1, N_COLS * 32), F32),
            pltpu.VMEM((N_COLS * 32, LANES), BF),
            pltpu.VMEM((Z * MSG, LANES), F32),
            pltpu.SemaphoreType.DMA((2,)),
            pltpu.SemaphoreType.DMA((2,)),
            pltpu.SemaphoreType.DMA((N_COLS,)),
            pltpu.SemaphoreType.DMA((N_COLS,)),
            pltpu.SemaphoreType.DMA((N_COLS,)),
            pltpu.SemaphoreType.DMA((N_COLS,)),
        ],
        compiler_params=pltpu.CompilerParams(
            collective_id=0, has_side_effects=True, vmem_limit_bytes=48 * 1024 * 1024
        ),
    )(
        rows, depth_kernel, point_weight, point_bias.reshape(1, C), vert_weight, vert_bias,
        exhaust, owner.reshape(1, E_DEV), cells.reshape(1, E_DEV),
    )
    return out.reshape(Z, MSG // YB, YB, LANES).transpose(0, 2, 1, 3).reshape(Z, YB, X * C // N_COLS)


def solution(mesh):
    placed = (
        P("cols", "rows", None),
        P(),
        P(),
        P(),
        P(),
        P(),
        P(("rows", "cols"), None),
        P(("rows", "cols"), None),
        P(("rows", "cols")),
    )
    return jax.shard_map(
        body, mesh=mesh, in_specs=placed, out_specs=P(None, "rows", "cols"), check_vma=False
    )
```

```python
import jax
import jax.numpy as jnp
from jax import lax
from jax.experimental import pallas as pl
from jax.experimental.pallas import tpu as pltpu
from jax.sharding import PartitionSpec as P

C = 32
X = 1024
Z = 32
YB = 4
KH = 7
KV = 9
LAYERS = 2
E_DEV = 512
N_ROWS = 16
N_COLS = 32
LANES = 128
TILES = X * C // LANES
TILE = TILES // N_COLS
MSG = YB * TILE
GROUPS = (1, 2, 3, 4)
MESH = pl.DeviceIdType.MESH
BF = jnp.bfloat16
F32 = jnp.float32
HIGH = lax.Precision.HIGHEST


def iota(shape, dim):
    return lax.broadcasted_iota(jnp.int32, shape, dim)


def dot(a, b):
    return jnp.dot(a, b, preferred_element_type=F32)


def select_matrix(rows, lanes):
    return iota((rows, lanes), 0) == iota((rows, lanes), 1) % rows


def lane_tile(x, lanes):
    return jnp.dot(
        x, select_matrix(C, lanes).astype(F32), preferred_element_type=F32, precision=HIGH
    )


def pack_exhaust(me, odd, ex_ref, own_ref, cell_ref, xs):
    owner = own_ref[...]
    cell = cell_ref[...]
    onehot = iota((N_COLS, E_DEV), 0) == owner
    before = (iota((E_DEV, E_DEV), 0) < iota((E_DEV, E_DEV), 1)).astype(F32).astype(BF)
    earlier = dot(onehot.astype(F32).astype(BF), before)
    rank = jnp.sum(jnp.where(onehot, earlier, 0.0), axis=0, keepdims=True)
    rank_i = rank.astype(jnp.int32)
    level = cell >> 7
    y = (cell >> 5) & 3
    x = cell & 31
    low = (y * odd + (3 - y) * (1 - odd)) * TILE + (x >> 2)
    zero = jnp.zeros((1, E_DEV), F32)
    values = jnp.concatenate(
        [level.astype(F32), low.astype(F32), (x & 3).astype(F32), rank, zero, zero, zero, zero],
        axis=0,
    )
    rank_col = jnp.transpose(values)[:, 3:4].astype(jnp.int32)
    lane = iota((E_DEV, LANES), 1)
    columns = ex_ref[...].astype(F32)
    tiled = jnp.transpose(jnp.concatenate([columns] * 4, axis=0))
    placed = jnp.where(lane // C == rank_col // 8, tiled, 0.0).astype(BF)
    row = iota((N_COLS * 8, E_DEV), 0)
    to_row = (row == owner * 8 + rank_i % 8).astype(F32).astype(BF)
    data = dot(to_row, placed)
    spread = jnp.broadcast_to(values[None], (N_COLS, 8, E_DEV)).reshape(N_COLS * 8, E_DEV)
    meta_rows = jnp.where(row // 8 == owner, spread, 0.0).astype(BF)
    meta_lane = (lane == rank_col + (me % 4) * 32).astype(F32).astype(BF)
    meta = dot(meta_rows, meta_lane)
    xs[...] = jnp.concatenate(
        [data.reshape(N_COLS, 8, LANES), meta.reshape(N_COLS, 8, LANES)], axis=1
    ).astype(BF)


def add_exhaust(xr, codes, rows_b, source):
    got = xr[...].astype(F32)
    data = got[:, :8, :].reshape(N_COLS * 8, LANES).astype(BF)
    m = iota((LANES, 4 * LANES), 0)
    n = iota((LANES, 4 * LANES), 1)
    expand = ((m // C == n // LANES) & (m % C == n % C)).astype(F32).astype(BF)
    wide = dot(data, expand)
    by_slot = jnp.concatenate(
        [wide[:, g * LANES : (g + 1) * LANES].reshape(N_COLS, 1, 8, LANES) for g in range(4)],
        axis=1,
    ).reshape(N_COLS * 32, LANES)
    lane = iota((LANES, LANES), 1)
    for b in range(8):
        meta = got[4 * b, 8:, :]
        for k in range(1, 4):
            meta = meta + got[4 * b + k, 8:, :]
        codes[:, b * LANES : (b + 1) * LANES] = meta[0:1] * 32.0 + meta[1:2]
        place = jnp.transpose(meta)[:, 2:3].astype(jnp.int32)
        rows_b[b * LANES : (b + 1) * LANES, :] = jnp.where(
            lane // C == place, by_slot[b * LANES : (b + 1) * LANES, :], 0.0
        ).astype(BF)

    @pl.loop(0, 4)
    def _(block):
        base = pl.multiple_of(block * 256, 256)
        row = (iota((256, N_COLS * 32), 0) + base).astype(F32)
        hit = (row == codes[...]).astype(F32).astype(BF)
        source[pl.ds(base, 256), :] = dot(hit, rows_b[...])


def horizontal_weights(dk_ref, pw_ref, dk_pad, hw):
    for i in range(KH):
        dk_pad[i * 8 : i * 8 + KH, 0:C] = dk_ref[i]
    columns = jnp.transpose(dk_pad[...])[0:C, :]
    point = dot(pw_ref[...], select_matrix(C, 2 * LANES).astype(F32).astype(BF))
    block = iota((C, 2 * LANES), 1) // C
    for i in range(KH):
        taps = jnp.zeros((C, 2 * LANES), F32)
        for m in range(KH):
            j = KH - 1 - m
            taps = jnp.where(block == m, columns[:, i * 8 + j : i * 8 + j + 1], taps)
        taps = jnp.concatenate([taps * point, jnp.zeros((C, LANES), F32)], axis=1)
        for cell in range(4):
            start = i * LANES + cell * C
            hw[start : start + C, :] = pltpu.roll(taps, (cell + 1) * C, 1).astype(BF)


def vertical_weights(vw_ref, vw_pad, vw):
    row = iota((LANES, LANES), 0)
    lane = iota((LANES, LANES), 1)
    for layer in range(LAYERS):
        taps = vw_ref[layer].astype(F32)
        for copy in range(4):
            vw_pad[copy * C : (copy + 1) * C, 0 : KV * C] = taps
        wide = jnp.transpose(vw_pad[...])
        for k in range(KV):
            part = wide[k * C : (k + 1) * C, :]
            whole = jnp.concatenate([part, part, part, part], axis=0)
            vw[layer, k * LANES : (k + 1) * LANES, :] = jnp.where(
                row // C == lane // C, whole, 0.0
            ).astype(BF)


def kernel(
    field_ref, dk_ref, pw_ref, pb_ref, vw_ref, vb_ref, ex_ref, own_ref, cell_ref, out_ref,
    stage, band, dk_pad, hw, vw_pad, vw, send, recv, mid, xs, xr, codes, rows_b, source,
    near_send, near_recv, far_send, far_recv, mix_send, mix_recv, ex_send, ex_recv,
):
    r = lax.axis_index("rows")
    me = lax.axis_index("cols")
    odd = lax.rem(r, 2)
    near = r + 1 - 2 * odd
    far = lax.rem(r + N_ROWS - 1 + 2 * odd, N_ROWS)
    has_far = jnp.logical_and(r > 0, r < N_ROWS - 1)
    barrier = pltpu.get_barrier_semaphore()

    for row in (near, far):
        pl.semaphore_signal(barrier, inc=1, device_id={"rows": row}, device_id_type=MESH)

    @pl.loop(1, N_COLS)
    def _(s):
        pl.semaphore_signal(
            barrier, inc=1, device_id={"cols": lax.rem(me + s, N_COLS)}, device_id_type=MESH
        )

    stage[...] = field_ref[...].astype(F32)
    for y in range(YB):
        band[3 + y] = stage[pl.ds(y, TILES, stride=YB), :].astype(BF)

    @pl.when(r == 0)
    def _():
        band[0:3] = jnp.zeros((3, TILES, LANES), BF)

    @pl.when(r == N_ROWS - 1)
    def _():
        band[7:10] = jnp.zeros((3, TILES, LANES), BF)

    pl.semaphore_wait(barrier, N_COLS + 1)

    near_copy = pltpu.make_async_remote_copy(
        src_ref=band.at[pl.ds(4 - odd, 3)], dst_ref=band.at[pl.ds(7 * odd, 3)],
        send_sem=near_send, recv_sem=near_recv, device_id={"rows": near}, device_id_type=MESH,
    )
    near_arrival = pltpu.make_async_remote_copy(
        src_ref=band.at[pl.ds(4 - odd, 3)], dst_ref=band.at[pl.ds(7 * (1 - odd), 3)],
        send_sem=near_send, recv_sem=near_recv, device_id={"rows": near}, device_id_type=MESH,
    )

    def far_copy(j):
        return pltpu.make_async_remote_copy(
            src_ref=band.at[odd * (7 - j) + (1 - odd) * (2 + j)],
            dst_ref=band.at[odd * (3 - j) + (1 - odd) * (6 + j)],
            send_sem=far_send.at[j - 1], recv_sem=far_recv.at[j - 1],
            device_id={"rows": far}, device_id_type=MESH,
        )

    def far_arrival(j):
        return pltpu.make_async_remote_copy(
            src_ref=band.at[odd * (7 - j) + (1 - odd) * (2 + j)],
            dst_ref=band.at[odd * (6 + j) + (1 - odd) * (3 - j)],
            send_sem=far_send.at[j - 1], recv_sem=far_recv.at[j - 1],
            device_id={"rows": far}, device_id_type=MESH,
        )

    @pl.when(has_far)
    def _():
        for j in range(1, 4):
            far_copy(j).start()

    near_copy.start()
    pack_exhaust(me, odd, ex_ref, own_ref, cell_ref, xs)

    @pl.loop(1, N_COLS)
    def _(s):
        there = lax.rem(me + s, N_COLS)
        pltpu.make_async_remote_copy(
            src_ref=xs.at[there], dst_ref=xr.at[me], send_sem=ex_send, recv_sem=ex_recv,
            device_id={"cols": there}, device_id_type=MESH,
        ).start()

    all_exhaust = pltpu.make_async_remote_copy(
        src_ref=xs.at[0 : N_COLS - 1], dst_ref=xr.at[0 : N_COLS - 1], send_sem=ex_send,
        recv_sem=ex_recv, device_id={"cols": lax.rem(me + 1, N_COLS)}, device_id_type=MESH,
    )
    all_mixed = pltpu.make_async_remote_copy(
        src_ref=send.at[0 : N_COLS - 1], dst_ref=recv.at[4 : N_COLS + 3], send_sem=mix_send,
        recv_sem=mix_recv, device_id={"cols": lax.rem(me + 1, N_COLS)}, device_id_type=MESH,
    )

    xr[me] = xs[me]
    horizontal_weights(dk_ref, pw_ref, dk_pad, hw)
    vertical_weights(vw_ref, vw_pad, vw)
    bias_h = lane_tile(pb_ref[...], LANES)
    bias_v = lane_tile(vb_ref[...], LANES)
    edge = jnp.zeros((4, MSG, LANES), BF)
    for buffer in (recv, mid):
        buffer[0:4] = edge
        buffer[4 + Z : 8 + Z] = edge

    row = iota((TILES, LANES), 0)

    def horizontal(slot):
        y = odd * slot + (1 - odd) * (3 - slot)
        rows = jnp.concatenate([band[y + i] for i in range(KH)], axis=1)
        parts = dot(rows, hw[...])
        right = pltpu.roll(parts[:, 0:LANES], TILES - 1, 0)
        left = pltpu.roll(parts[:, 2 * LANES : 3 * LANES], 1, 0)
        total = (
            parts[:, LANES : 2 * LANES]
            + jnp.where(row < TILES - 1, right, 0.0)
            + jnp.where(row > 0, left, 0.0)
        )
        mixed = band[3 + y].astype(F32) + jax.nn.gelu(total + bias_h)
        send[:, slot * TILE : (slot + 1) * TILE, :] = mixed.astype(BF).reshape(N_COLS, TILE, LANES)

    near_arrival.wait_recv()
    first = 0
    for slot in range(YB):
        if slot > 0:

            @pl.when(has_far)
            def _():
                far_arrival(slot).wait_recv()

        horizontal(slot)
        if slot + 1 in GROUPS:
            part = slice(first * TILE, (slot + 1) * TILE)
            first = slot + 1

            @pl.loop(1, N_COLS)
            def _(s):
                there = lax.rem(me + s, N_COLS)
                pltpu.make_async_remote_copy(
                    src_ref=send.at[there, part], dst_ref=recv.at[4 + me, part],
                    send_sem=mix_send, recv_sem=mix_recv, device_id={"cols": there},
                    device_id_type=MESH,
                ).start()

    recv[4 + me] = send[me]
    all_exhaust.wait_recv()
    add_exhaust(xr, codes, rows_b, source)
    all_mixed.wait_recv()

    def conv(buffer, layer, block):
        rows = jnp.concatenate(
            [buffer[pl.ds(block * 8 + k, 8)].reshape(8 * MSG, LANES) for k in range(KV)], axis=1
        )
        before = buffer[pl.ds(block * 8 + 4, 8)].reshape(8 * MSG, LANES).astype(F32)
        return before + jax.nn.gelu(dot(rows, vw[layer]) + bias_v[layer : layer + 1])

    @pl.loop(0, 4)
    def _(block):
        mid[pl.ds(block * 8 + 4, 8)] = conv(recv, 0, block).astype(BF).reshape(8, MSG, LANES)

    @pl.loop(0, 4)
    def _(block):
        base = pl.multiple_of(block * 256, 256)
        result = conv(mid, 1, block) + source[pl.ds(base, 256), :]
        for level in range(8):
            for slot in range(YB):
                y = odd * slot + (1 - odd) * (3 - slot)
                start = level * MSG + slot * TILE
                stage[pl.ds(base + level * MSG + y, TILE, stride=YB), :] = result[
                    start : start + TILE
                ]
        out_ref[pl.ds(base, 256), :] = stage[pl.ds(base, 256), :].astype(BF)

    near_copy.wait_send()

    @pl.when(has_far)
    def _():
        for j in range(1, 4):
            far_copy(j).wait_send()

    all_exhaust.wait_send()
    all_mixed.wait_send()


def body(
    field, depth_kernel, point_weight, point_bias, vert_weight, vert_bias, exhaust, owner, cells
):
    rows = field.reshape(YB, TILES, LANES).transpose(1, 0, 2).reshape(TILES * YB, LANES)
    out = pl.pallas_call(
        kernel,
        out_shape=jax.ShapeDtypeStruct((Z * MSG, LANES), BF),
        in_specs=[pl.BlockSpec(memory_space=pltpu.VMEM)] * 9,
        out_specs=pl.BlockSpec(memory_space=pltpu.VMEM),
        scratch_shapes=[
            pltpu.VMEM((TILES * YB, LANES), F32),
            pltpu.VMEM((YB + 6, TILES, LANES), BF),
            pltpu.VMEM((LANES, LANES), F32),
            pltpu.VMEM((KH * LANES, 3 * LANES), BF),
            pltpu.VMEM((LANES, 3 * LANES), F32),
            pltpu.VMEM((LAYERS, KV * LANES, LANES), BF),
            pltpu.VMEM((N_COLS, MSG, LANES), BF),
            pltpu.VMEM((Z + 8, MSG, LANES), BF),
            pltpu.VMEM((Z + 8, MSG, LANES), BF),
            pltpu.VMEM((N_COLS, 16, LANES), BF),
            pltpu.VMEM((N_COLS, 16, LANES), BF),
            pltpu.VMEM((1, N_COLS * 32), F32),
            pltpu.VMEM((N_COLS * 32, LANES), BF),
            pltpu.VMEM((Z * MSG, LANES), F32),
            pltpu.SemaphoreType.DMA,
            pltpu.SemaphoreType.DMA,
            pltpu.SemaphoreType.DMA((3,)),
            pltpu.SemaphoreType.DMA((3,)),
            pltpu.SemaphoreType.DMA,
            pltpu.SemaphoreType.DMA,
            pltpu.SemaphoreType.DMA,
            pltpu.SemaphoreType.DMA,
        ],
        compiler_params=pltpu.CompilerParams(
            collective_id=0, has_side_effects=True, vmem_limit_bytes=48 * 1024 * 1024
        ),
    )(
        rows, depth_kernel, point_weight, point_bias.reshape(1, C),
        vert_weight.transpose(0, 2, 1), vert_bias, exhaust.T, owner.reshape(1, E_DEV), cells.reshape(1, E_DEV),
    )
    return out.reshape(Z, MSG // YB, YB, LANES).transpose(0, 2, 1, 3).reshape(Z, YB, X * C // N_COLS)


def solution(mesh):
    placed = (
        P("cols", "rows", None),
        P(),
        P(),
        P(),
        P(),
        P(),
        P(("rows", "cols"), None),
        P(("rows", "cols"), None),
        P(("rows", "cols")),
    )
    return jax.shard_map(
        body, mesh=mesh, in_specs=placed, out_specs=P(None, "rows", "cols"), check_vma=False
    )
```

```python
import jax
import jax.numpy as jnp
from jax import lax
from jax.experimental import pallas as pl
from jax.experimental.pallas import tpu as pltpu
from jax.sharding import PartitionSpec as P

C = 32
X = 1024
Z = 32
YB = 4
KH = 7
KV = 9
LAYERS = 2
E_DEV = 512
N_ROWS = 16
N_COLS = 32
LANES = 128
TILES = X * C // LANES
TILE = TILES // N_COLS
MSG = YB * TILE
GROUPS = (2, 4)
N_Z = 8
HUB = 15
LATE = 4
MESH = pl.DeviceIdType.MESH
BF = jnp.bfloat16
F32 = jnp.float32
HIGH = lax.Precision.HIGHEST


def iota(shape, dim):
    return lax.broadcasted_iota(jnp.int32, shape, dim)


def dot(a, b):
    return jnp.dot(a, b, preferred_element_type=F32)


def select_matrix(rows, lanes):
    return iota((rows, lanes), 0) == iota((rows, lanes), 1) % rows


def lane_tile(x, lanes):
    return jnp.dot(
        x, select_matrix(C, lanes).astype(F32), preferred_element_type=F32, precision=HIGH
    )


def pack_exhaust(me, odd, ex_ref, own_ref, cell_ref, xs):
    owner = own_ref[...]
    cell = cell_ref[...]
    onehot = iota((N_COLS, E_DEV), 0) == owner
    before = (iota((E_DEV, E_DEV), 0) < iota((E_DEV, E_DEV), 1)).astype(F32).astype(BF)
    earlier = dot(onehot.astype(F32).astype(BF), before)
    rank = jnp.sum(jnp.where(onehot, earlier, 0.0), axis=0, keepdims=True)
    rank_i = rank.astype(jnp.int32)
    level = cell >> 7
    y = (cell >> 5) & 3
    x = cell & 31
    low = (y * odd + (3 - y) * (1 - odd)) * TILE + (x >> 2)
    zero = jnp.zeros((1, E_DEV), F32)
    values = jnp.concatenate(
        [level.astype(F32), low.astype(F32), (x & 3).astype(F32), rank, zero, zero, zero, zero],
        axis=0,
    )
    rank_col = jnp.transpose(values)[:, 3:4].astype(jnp.int32)
    lane = iota((E_DEV, LANES), 1)
    columns = ex_ref[...].astype(F32)
    tiled = jnp.transpose(jnp.concatenate([columns] * 4, axis=0))
    placed = jnp.where(lane // C == rank_col // 8, tiled, 0.0).astype(BF)
    row = iota((N_COLS * 8, E_DEV), 0)
    to_row = (row == owner * 8 + rank_i % 8).astype(F32).astype(BF)
    data = dot(to_row, placed)
    spread = jnp.broadcast_to(values[None], (N_COLS, 8, E_DEV)).reshape(N_COLS * 8, E_DEV)
    meta_rows = jnp.where(row // 8 == owner, spread, 0.0).astype(BF)
    meta_lane = (lane == rank_col + (me % 4) * 32).astype(F32).astype(BF)
    meta = dot(meta_rows, meta_lane)
    xs[...] = jnp.concatenate(
        [data.reshape(N_COLS, 8, LANES), meta.reshape(N_COLS, 8, LANES)], axis=1
    ).astype(BF)


def add_exhaust(xr, codes, rows_b, source):
    got = xr[...].astype(F32)
    data = got[:, :8, :].reshape(N_COLS * 8, LANES).astype(BF)
    m = iota((LANES, 4 * LANES), 0)
    n = iota((LANES, 4 * LANES), 1)
    expand = ((m // C == n // LANES) & (m % C == n % C)).astype(F32).astype(BF)
    wide = dot(data, expand)
    by_slot = jnp.concatenate(
        [wide[:, g * LANES : (g + 1) * LANES].reshape(N_COLS, 1, 8, LANES) for g in range(4)],
        axis=1,
    ).reshape(N_COLS * 32, LANES)
    lane = iota((LANES, LANES), 1)
    for b in range(8):
        meta = got[4 * b, 8:, :]
        for k in range(1, 4):
            meta = meta + got[4 * b + k, 8:, :]
        codes[:, b * LANES : (b + 1) * LANES] = meta[0:1] * 32.0 + meta[1:2]
        place = jnp.transpose(meta)[:, 2:3].astype(jnp.int32)
        rows_b[b * LANES : (b + 1) * LANES, :] = jnp.where(
            lane // C == place, by_slot[b * LANES : (b + 1) * LANES, :], 0.0
        ).astype(BF)

    @pl.loop(0, 4)
    def _(block):
        base = pl.multiple_of(block * 256, 256)
        row = (iota((256, N_COLS * 32), 0) + base).astype(F32)
        hit = (row == codes[...]).astype(F32).astype(BF)
        source[pl.ds(base, 256), :] = dot(hit, rows_b[...])


def horizontal_weights(dk_ref, pw_ref, dk_pad, hw):
    for i in range(KH):
        dk_pad[i * 8 : i * 8 + KH, 0:C] = dk_ref[i]
    columns = jnp.transpose(dk_pad[...])[0:C, :]
    point = dot(pw_ref[...], select_matrix(C, 2 * LANES).astype(F32).astype(BF))
    block = iota((C, 2 * LANES), 1) // C
    for i in range(KH):
        taps = jnp.zeros((C, 2 * LANES), F32)
        for m in range(KH):
            j = KH - 1 - m
            taps = jnp.where(block == m, columns[:, i * 8 + j : i * 8 + j + 1], taps)
        taps = jnp.concatenate([taps * point, jnp.zeros((C, LANES), F32)], axis=1)
        for cell in range(4):
            start = i * LANES + cell * C
            hw[start : start + C, :] = pltpu.roll(taps, (cell + 1) * C, 1).astype(BF)


def vertical_weights(vw_ref, vw_pad, vw):
    row = iota((LANES, LANES), 0)
    lane = iota((LANES, LANES), 1)
    for layer in range(LAYERS):
        taps = vw_ref[layer].astype(F32)
        for copy in range(4):
            vw_pad[copy * C : (copy + 1) * C, 0 : KV * C] = taps
        wide = jnp.transpose(vw_pad[...])
        for k in range(KV):
            part = wide[k * C : (k + 1) * C, :]
            whole = jnp.concatenate([part, part, part, part], axis=0)
            vw[layer, k * LANES : (k + 1) * LANES, :] = jnp.where(
                row // C == lane // C, whole, 0.0
            ).astype(BF)


def kernel(
    field_hbm, dk_hbm, pw_hbm, pb_hbm, vw_hbm, vb_hbm, ex_hbm, own_hbm, cell_hbm, out_ref,
    field_ref, dk_ref, pw_ref, pb_ref, vw_ref, vb_ref, ex_ref, own_ref, cell_ref, stage, band, dk_pad, hw, vw_pad, vw, send, recv, mid, xs, xr, codes, rows_b, source,
    near_send, near_recv, far_send, far_recv, mix_send, mix_recv, ex_send, ex_recv, go, load,
):
    r = lax.axis_index("rows")
    me = lax.axis_index("cols")
    odd = lax.rem(r, 2)
    near = r + 1 - 2 * odd
    far = lax.rem(r + N_ROWS - 1 + 2 * odd, N_ROWS)
    has_far = jnp.logical_and(r > 0, r < N_ROWS - 1)
    barrier = pltpu.get_barrier_semaphore()
    loads = [
        pltpu.make_async_copy(source_ref, target_ref, load.at[i])
        for i, (source_ref, target_ref) in enumerate(
            (
                (field_hbm, field_ref), (ex_hbm, ex_ref), (own_hbm, own_ref), (cell_hbm, cell_ref),
                (dk_hbm, dk_ref), (pw_hbm, pw_ref), (pb_hbm, pb_ref), (vw_hbm, vw_ref),
                (vb_hbm, vb_ref),
            )
        )
    ]
    for copy in loads:
        copy.start()

    for row in (near, far):
        pl.semaphore_signal(barrier, inc=1, device_id={"rows": row}, device_id_type=MESH)

    @pl.when(me != HUB)
    def _():
        pl.semaphore_signal(barrier, inc=1, device_id={"cols": HUB}, device_id_type=MESH)

    loads[0].wait()
    stage[...] = field_ref[...].astype(F32)
    for y in range(YB):
        band[3 + y] = stage[pl.ds(y, TILES, stride=YB), :].astype(BF)

    @pl.when(r == 0)
    def _():
        band[0:3] = jnp.zeros((3, TILES, LANES), BF)

    @pl.when(r == N_ROWS - 1)
    def _():
        band[7:10] = jnp.zeros((3, TILES, LANES), BF)

    @pl.when(me == HUB)
    def _():
        pl.semaphore_wait(barrier, N_COLS + 1)

        @pl.loop(1, N_COLS)
        def _(s):
            pl.semaphore_signal(
                go, inc=1, device_id={"cols": lax.rem(me + s, N_COLS)}, device_id_type=MESH
            )

    @pl.when(me != HUB)
    def _():
        pl.semaphore_wait(barrier, 2)

    near_copy = pltpu.make_async_remote_copy(
        src_ref=band.at[pl.ds(4 - odd, 3)], dst_ref=band.at[pl.ds(7 * odd, 3)],
        send_sem=near_send, recv_sem=near_recv, device_id={"rows": near}, device_id_type=MESH,
    )
    near_arrival = pltpu.make_async_remote_copy(
        src_ref=band.at[pl.ds(4 - odd, 3)], dst_ref=band.at[pl.ds(7 * (1 - odd), 3)],
        send_sem=near_send, recv_sem=near_recv, device_id={"rows": near}, device_id_type=MESH,
    )

    def far_copy(j):
        return pltpu.make_async_remote_copy(
            src_ref=band.at[odd * (7 - j) + (1 - odd) * (2 + j)],
            dst_ref=band.at[odd * (3 - j) + (1 - odd) * (6 + j)],
            send_sem=far_send.at[j - 1], recv_sem=far_recv.at[j - 1],
            device_id={"rows": far}, device_id_type=MESH,
        )

    def far_arrival(j):
        return pltpu.make_async_remote_copy(
            src_ref=band.at[odd * (7 - j) + (1 - odd) * (2 + j)],
            dst_ref=band.at[odd * (6 + j) + (1 - odd) * (3 - j)],
            send_sem=far_send.at[j - 1], recv_sem=far_recv.at[j - 1],
            device_id={"rows": far}, device_id_type=MESH,
        )

    @pl.when(has_far)
    def _():
        for j in range(1, 4):
            far_copy(j).start()

    near_copy.start()
    for copy in loads[1:]:
        copy.wait()
    pack_exhaust(me, odd, ex_ref, own_ref, cell_ref, xs)

    def await_go():
        @pl.when(me != HUB)
        def _():
            pl.semaphore_wait(go, 1)

    def send_exhaust():
        @pl.loop(1, N_COLS)
        def _(s):
            there = lax.rem(me + s, N_COLS)
            pltpu.make_async_remote_copy(
                src_ref=xs.at[there], dst_ref=xr.at[me], send_sem=ex_send, recv_sem=ex_recv,
                device_id={"cols": there}, device_id_type=MESH,
            ).start()

    all_exhaust = pltpu.make_async_remote_copy(
        src_ref=xs.at[0 : N_COLS - 1], dst_ref=xr.at[0 : N_COLS - 1], send_sem=ex_send,
        recv_sem=ex_recv, device_id={"cols": lax.rem(me + 1, N_COLS)}, device_id_type=MESH,
    )
    all_mixed = pltpu.make_async_remote_copy(
        src_ref=send.at[0 : N_COLS - 1], dst_ref=recv.at[4 : N_COLS + 3], send_sem=mix_send,
        recv_sem=mix_recv, device_id={"cols": lax.rem(me + 1, N_COLS)}, device_id_type=MESH,
    )

    xr[me] = xs[me]
    horizontal_weights(dk_ref, pw_ref, dk_pad, hw)
    vertical_weights(vw_ref, vw_pad, vw)
    bias_h = lane_tile(pb_ref[...], LANES)
    bias_v = lane_tile(vb_ref[...], LANES)
    edge = jnp.zeros((4, MSG, LANES), BF)
    for buffer in (recv, mid):
        buffer[0:4] = edge
        buffer[4 + Z : 8 + Z] = edge

    row = iota((TILES, LANES), 0)

    def horizontal(slot):
        y = odd * slot + (1 - odd) * (3 - slot)
        rows = jnp.concatenate([band[y + i] for i in range(KH)], axis=1)
        parts = dot(rows, hw[...])
        right = pltpu.roll(parts[:, 0:LANES], TILES - 1, 0)
        left = pltpu.roll(parts[:, 2 * LANES : 3 * LANES], 1, 0)
        total = (
            parts[:, LANES : 2 * LANES]
            + jnp.where(row < TILES - 1, right, 0.0)
            + jnp.where(row > 0, left, 0.0)
        )
        mixed = band[3 + y].astype(F32) + jax.nn.gelu(total + bias_h)
        send[:, slot * TILE : (slot + 1) * TILE, :] = mixed.astype(BF).reshape(N_COLS, TILE, LANES)

    late = lax.rem(me, N_Z) >= LATE

    @pl.when(late)
    def _():
        await_go()
        send_exhaust()

    near_arrival.wait_recv()
    first = 0
    for slot in range(YB):
        if slot > 0:

            @pl.when(has_far)
            def _():
                far_arrival(slot).wait_recv()

        horizontal(slot)
        if slot + 1 == GROUPS[0]:

            @pl.when(jnp.logical_not(late))
            def _():
                await_go()
                send_exhaust()

        if slot + 1 in GROUPS:
            part = slice(first * TILE, (slot + 1) * TILE)
            first = slot + 1

            @pl.loop(1, N_COLS)
            def _(s):
                there = lax.rem(me + s, N_COLS)
                pltpu.make_async_remote_copy(
                    src_ref=send.at[there, part], dst_ref=recv.at[4 + me, part],
                    send_sem=mix_send, recv_sem=mix_recv, device_id={"cols": there},
                    device_id_type=MESH,
                ).start()

    recv[4 + me] = send[me]
    all_exhaust.wait_recv()
    add_exhaust(xr, codes, rows_b, source)
    all_mixed.wait_recv()

    def conv(buffer, layer, block):
        rows = jnp.concatenate(
            [buffer[pl.ds(block * 8 + k, 8)].reshape(8 * MSG, LANES) for k in range(KV)], axis=1
        )
        before = buffer[pl.ds(block * 8 + 4, 8)].reshape(8 * MSG, LANES).astype(F32)
        return before + jax.nn.gelu(dot(rows, vw[layer]) + bias_v[layer : layer + 1])

    @pl.loop(0, 4)
    def _(block):
        mid[pl.ds(block * 8 + 4, 8)] = conv(recv, 0, block).astype(BF).reshape(8, MSG, LANES)

    @pl.loop(0, 4)
    def _(block):
        base = pl.multiple_of(block * 256, 256)
        result = conv(mid, 1, block) + source[pl.ds(base, 256), :]
        for level in range(8):
            for slot in range(YB):
                y = odd * slot + (1 - odd) * (3 - slot)
                start = level * MSG + slot * TILE
                stage[pl.ds(base + level * MSG + y, TILE, stride=YB), :] = result[
                    start : start + TILE
                ]
        out_ref[pl.ds(base, 256), :] = stage[pl.ds(base, 256), :].astype(BF)

    near_copy.wait_send()

    @pl.when(has_far)
    def _():
        for j in range(1, 4):
            far_copy(j).wait_send()

    all_exhaust.wait_send()
    all_mixed.wait_send()


def body(
    field, depth_kernel, point_weight, point_bias, vert_weight, vert_bias, exhaust, owner, cells
):
    rows = field.reshape(YB, TILES, LANES).transpose(1, 0, 2).reshape(TILES * YB, LANES)
    out = pl.pallas_call(
        kernel,
        out_shape=jax.ShapeDtypeStruct((Z * MSG, LANES), BF),
        in_specs=[pl.BlockSpec(memory_space=pltpu.HBM)] * 9,
        out_specs=pl.BlockSpec(memory_space=pltpu.VMEM),
        scratch_shapes=[
            pltpu.VMEM((TILES * YB, LANES), BF),
            pltpu.VMEM((KH, KH, C), F32),
            pltpu.VMEM((C, C), BF),
            pltpu.VMEM((1, C), F32),
            pltpu.VMEM((LAYERS, C, KV * C), BF),
            pltpu.VMEM((LAYERS, C), F32),
            pltpu.VMEM((C, E_DEV), BF),
            pltpu.VMEM((1, E_DEV), jnp.int32),
            pltpu.VMEM((1, E_DEV), jnp.int32),
            pltpu.VMEM((TILES * YB, LANES), F32),
            pltpu.VMEM((YB + 6, TILES, LANES), BF),
            pltpu.VMEM((LANES, LANES), F32),
            pltpu.VMEM((KH * LANES, 3 * LANES), BF),
            pltpu.VMEM((LANES, 3 * LANES), F32),
            pltpu.VMEM((LAYERS, KV * LANES, LANES), BF),
            pltpu.VMEM((N_COLS, MSG, LANES), BF),
            pltpu.VMEM((Z + 8, MSG, LANES), BF),
            pltpu.VMEM((Z + 8, MSG, LANES), BF),
            pltpu.VMEM((N_COLS, 16, LANES), BF),
            pltpu.VMEM((N_COLS, 16, LANES), BF),
            pltpu.VMEM((1, N_COLS * 32), F32),
            pltpu.VMEM((N_COLS * 32, LANES), BF),
            pltpu.VMEM((Z * MSG, LANES), F32),
            pltpu.SemaphoreType.DMA,
            pltpu.SemaphoreType.DMA,
            pltpu.SemaphoreType.DMA((3,)),
            pltpu.SemaphoreType.DMA((3,)),
            pltpu.SemaphoreType.DMA,
            pltpu.SemaphoreType.DMA,
            pltpu.SemaphoreType.DMA,
            pltpu.SemaphoreType.DMA,
            pltpu.SemaphoreType.REGULAR,
            pltpu.SemaphoreType.DMA((9,)),
        ],
        compiler_params=pltpu.CompilerParams(
            collective_id=0, has_side_effects=True, vmem_limit_bytes=48 * 1024 * 1024
        ),
    )(
        *(
            pltpu.with_memory_space_constraint(a, pltpu.HBM)
            for a in (
        rows, depth_kernel, point_weight, point_bias.reshape(1, C),
        vert_weight.transpose(0, 2, 1), vert_bias, exhaust.T, owner.reshape(1, E_DEV), cells.reshape(1, E_DEV),
            )
        )
    )
    return out.reshape(Z, MSG // YB, YB, LANES).transpose(0, 2, 1, 3).reshape(Z, YB, X * C // N_COLS)


def solution(mesh):
    placed = (
        P("cols", "rows", None),
        P(),
        P(),
        P(),
        P(),
        P(),
        P(("rows", "cols"), None),
        P(("rows", "cols"), None),
        P(("rows", "cols")),
    )
    return jax.shard_map(
        body, mesh=mesh, in_specs=placed, out_specs=P(None, "rows", "cols"), check_vma=False
    )
```

```python
import jax
import jax.numpy as jnp
from jax import lax
from jax.experimental import pallas as pl
from jax.experimental.pallas import tpu as pltpu
from jax.sharding import PartitionSpec as P

C = 32
X = 1024
Z = 32
YB = 4
KH = 7
KV = 9
LAYERS = 2
E_DEV = 512
N_ROWS = 16
N_COLS = 32
LANES = 128
TILES = X * C // LANES
TILE = TILES // N_COLS
MSG = YB * TILE
GROUPS = (2, 4)
N_Z = 8
HUB = 15
PAIRS = 16
LATE = 4
MESH = pl.DeviceIdType.MESH
BF = jnp.bfloat16
F32 = jnp.float32
HIGH = lax.Precision.HIGHEST


def iota(shape, dim):
    return lax.broadcasted_iota(jnp.int32, shape, dim)


def dot(a, b):
    return jnp.dot(a, b, preferred_element_type=F32)


def select_matrix(rows, lanes):
    return iota((rows, lanes), 0) == iota((rows, lanes), 1) % rows


def lane_tile(x, lanes):
    return jnp.dot(
        x, select_matrix(C, lanes).astype(F32), preferred_element_type=F32, precision=HIGH
    )


def pack_exhaust(me, odd, ex_ref, own_ref, cell_ref, xs):
    owner = own_ref[...]
    cell = cell_ref[...]
    onehot = iota((N_COLS, E_DEV), 0) == owner
    before = (iota((E_DEV, E_DEV), 0) < iota((E_DEV, E_DEV), 1)).astype(F32).astype(BF)
    earlier = dot(onehot.astype(F32).astype(BF), before)
    rank = jnp.sum(jnp.where(onehot, earlier, 0.0), axis=0, keepdims=True)
    rank_i = rank.astype(jnp.int32)
    level = cell >> 7
    y = (cell >> 5) & 3
    x = cell & 31
    low = (y * odd + (3 - y) * (1 - odd)) * TILE + (x >> 2)
    zero = jnp.zeros((1, E_DEV), F32)
    values = jnp.concatenate(
        [level.astype(F32), low.astype(F32), (x & 3).astype(F32), rank, zero, zero, zero, zero],
        axis=0,
    )
    rank_col = jnp.transpose(values)[:, 3:4].astype(jnp.int32)
    lane = iota((E_DEV, LANES), 1)
    columns = ex_ref[...].astype(F32)
    tiled = jnp.transpose(jnp.concatenate([columns] * 4, axis=0))
    placed = jnp.where(lane // C == rank_col // 8, tiled, 0.0).astype(BF)
    row = iota((N_COLS * 8, E_DEV), 0)
    to_row = (row == owner * 8 + rank_i % 8).astype(F32).astype(BF)
    data = dot(to_row, placed)
    spread = jnp.broadcast_to(values[None], (N_COLS, 8, E_DEV)).reshape(N_COLS * 8, E_DEV)
    meta_rows = jnp.where(row // 8 == owner, spread, 0.0).astype(BF)
    meta_lane = (lane == rank_col + (me % 4) * 32).astype(F32).astype(BF)
    meta = dot(meta_rows, meta_lane)
    xs[...] = jnp.concatenate(
        [data.reshape(N_COLS, 8, LANES), meta.reshape(N_COLS, 8, LANES)], axis=1
    ).astype(BF)


def add_exhaust(xr, codes, rows_b, source):
    got = xr[...].astype(F32)
    data = got[:, :8, :].reshape(N_COLS * 8, LANES).astype(BF)
    m = iota((LANES, 4 * LANES), 0)
    n = iota((LANES, 4 * LANES), 1)
    expand = ((m // C == n // LANES) & (m % C == n % C)).astype(F32).astype(BF)
    wide = dot(data, expand)
    by_slot = jnp.concatenate(
        [wide[:, g * LANES : (g + 1) * LANES].reshape(N_COLS, 1, 8, LANES) for g in range(4)],
        axis=1,
    ).reshape(N_COLS * 32, LANES)
    lane = iota((LANES, LANES), 1)
    for b in range(8):
        meta = got[4 * b, 8:, :]
        for k in range(1, 4):
            meta = meta + got[4 * b + k, 8:, :]
        codes[:, b * LANES : (b + 1) * LANES] = meta[0:1] * 32.0 + meta[1:2]
        place = jnp.transpose(meta)[:, 2:3].astype(jnp.int32)
        rows_b[b * LANES : (b + 1) * LANES, :] = jnp.where(
            lane // C == place, by_slot[b * LANES : (b + 1) * LANES, :], 0.0
        ).astype(BF)

    @pl.loop(0, 4)
    def _(block):
        base = pl.multiple_of(block * 256, 256)
        row = (iota((256, N_COLS * 32), 0) + base).astype(F32)
        hit = (row == codes[...]).astype(F32).astype(BF)
        source[pl.ds(base, 256), :] = dot(hit, rows_b[...])


def horizontal_weights(dk_ref, pw_ref, dk_pad, hw):
    for i in range(KH):
        dk_pad[i * 8 : i * 8 + KH, 0:C] = dk_ref[i]
    columns = jnp.transpose(dk_pad[...])[0:C, :]
    point = dot(pw_ref[...], select_matrix(C, 2 * LANES).astype(F32).astype(BF))
    block = iota((C, 2 * LANES), 1) // C
    for i in range(KH):
        taps = jnp.zeros((C, 2 * LANES), F32)
        for m in range(KH):
            j = KH - 1 - m
            taps = jnp.where(block == m, columns[:, i * 8 + j : i * 8 + j + 1], taps)
        taps = jnp.concatenate([taps * point, jnp.zeros((C, LANES), F32)], axis=1)
        for cell in range(4):
            start = i * LANES + cell * C
            hw[start : start + C, :] = pltpu.roll(taps, (cell + 1) * C, 1).astype(BF)


def vertical_weights(vw_ref, vw_pad, vw):
    row = iota((LANES, LANES), 0)
    lane = iota((LANES, LANES), 1)
    for layer in range(LAYERS):
        taps = vw_ref[layer].astype(F32)
        for copy in range(4):
            vw_pad[copy * C : (copy + 1) * C, 0 : KV * C] = taps
        wide = jnp.transpose(vw_pad[...])
        for k in range(KV):
            part = wide[k * C : (k + 1) * C, :]
            whole = jnp.concatenate([part, part, part, part], axis=0)
            block = jnp.where(row // C == lane // C, whole, 0.0).astype(BF)
            vw[layer, k * LANES : (k + 1) * LANES, 0:LANES] = block
            vw[layer, (k + 1) * LANES : (k + 2) * LANES, LANES : 2 * LANES] = block
        empty = jnp.zeros((LANES, LANES), BF)
        vw[layer, KV * LANES : (KV + 1) * LANES, 0:LANES] = empty
        vw[layer, 0:LANES, LANES : 2 * LANES] = empty


def kernel(
    field_hbm, dk_hbm, pw_hbm, pb_hbm, vw_hbm, vb_hbm, ex_hbm, own_hbm, cell_hbm, out_ref,
    field_ref, dk_ref, pw_ref, pb_ref, vw_ref, vb_ref, ex_ref, own_ref, cell_ref, stage, band, dk_pad, hw, vw_pad, vw, send, recv, mid, xs, xr, codes, rows_b, source,
    near_send, near_recv, far_send, far_recv, mix_send, mix_recv, ex_send, ex_recv, go, load,
):
    r = lax.axis_index("rows")
    me = lax.axis_index("cols")
    odd = lax.rem(r, 2)
    near = r + 1 - 2 * odd
    far = lax.rem(r + N_ROWS - 1 + 2 * odd, N_ROWS)
    has_far = jnp.logical_and(r > 0, r < N_ROWS - 1)
    barrier = pltpu.get_barrier_semaphore()
    loads = [
        pltpu.make_async_copy(source_ref, target_ref, load.at[i])
        for i, (source_ref, target_ref) in enumerate(
            (
                (field_hbm, field_ref), (ex_hbm, ex_ref), (own_hbm, own_ref), (cell_hbm, cell_ref),
                (dk_hbm, dk_ref), (pw_hbm, pw_ref), (pb_hbm, pb_ref), (vw_hbm, vw_ref),
                (vb_hbm, vb_ref),
            )
        )
    ]
    for copy in loads:
        copy.start()

    for row in (near, far):
        pl.semaphore_signal(barrier, inc=1, device_id={"rows": row}, device_id_type=MESH)

    @pl.when(me != HUB)
    def _():
        pl.semaphore_signal(barrier, inc=1, device_id={"cols": HUB}, device_id_type=MESH)

    loads[0].wait()
    stage[...] = field_ref[...].astype(F32)
    for y in range(YB):
        band[3 + y] = stage[pl.ds(y, TILES, stride=YB), :].astype(BF)

    @pl.when(r == 0)
    def _():
        band[0:3] = jnp.zeros((3, TILES, LANES), BF)

    @pl.when(r == N_ROWS - 1)
    def _():
        band[7:10] = jnp.zeros((3, TILES, LANES), BF)

    @pl.when(me == HUB)
    def _():
        pl.semaphore_wait(barrier, N_COLS + 1)

        @pl.loop(1, N_COLS)
        def _(s):
            pl.semaphore_signal(
                go, inc=1, device_id={"cols": lax.rem(me + s, N_COLS)}, device_id_type=MESH
            )

    @pl.when(me != HUB)
    def _():
        pl.semaphore_wait(barrier, 2)

    near_copy = pltpu.make_async_remote_copy(
        src_ref=band.at[pl.ds(4 - odd, 3)], dst_ref=band.at[pl.ds(7 * odd, 3)],
        send_sem=near_send, recv_sem=near_recv, device_id={"rows": near}, device_id_type=MESH,
    )
    near_arrival = pltpu.make_async_remote_copy(
        src_ref=band.at[pl.ds(4 - odd, 3)], dst_ref=band.at[pl.ds(7 * (1 - odd), 3)],
        send_sem=near_send, recv_sem=near_recv, device_id={"rows": near}, device_id_type=MESH,
    )

    def far_copy(j):
        return pltpu.make_async_remote_copy(
            src_ref=band.at[odd * (7 - j) + (1 - odd) * (2 + j)],
            dst_ref=band.at[odd * (3 - j) + (1 - odd) * (6 + j)],
            send_sem=far_send.at[j - 1], recv_sem=far_recv.at[j - 1],
            device_id={"rows": far}, device_id_type=MESH,
        )

    def far_arrival(j):
        return pltpu.make_async_remote_copy(
            src_ref=band.at[odd * (7 - j) + (1 - odd) * (2 + j)],
            dst_ref=band.at[odd * (6 + j) + (1 - odd) * (3 - j)],
            send_sem=far_send.at[j - 1], recv_sem=far_recv.at[j - 1],
            device_id={"rows": far}, device_id_type=MESH,
        )

    @pl.when(has_far)
    def _():
        for j in range(1, 4):
            far_copy(j).start()

    near_copy.start()
    for copy in loads[1:]:
        copy.wait()
    pack_exhaust(me, odd, ex_ref, own_ref, cell_ref, xs)

    def await_go():
        @pl.when(me != HUB)
        def _():
            pl.semaphore_wait(go, 1)

    def send_exhaust():
        @pl.loop(1, N_COLS)
        def _(s):
            there = lax.rem(me + s, N_COLS)
            pltpu.make_async_remote_copy(
                src_ref=xs.at[there], dst_ref=xr.at[me], send_sem=ex_send, recv_sem=ex_recv,
                device_id={"cols": there}, device_id_type=MESH,
            ).start()

    all_exhaust = pltpu.make_async_remote_copy(
        src_ref=xs.at[0 : N_COLS - 1], dst_ref=xr.at[0 : N_COLS - 1], send_sem=ex_send,
        recv_sem=ex_recv, device_id={"cols": lax.rem(me + 1, N_COLS)}, device_id_type=MESH,
    )
    all_mixed = pltpu.make_async_remote_copy(
        src_ref=send.at[0 : N_COLS - 1], dst_ref=recv.at[4 : N_COLS + 3], send_sem=mix_send,
        recv_sem=mix_recv, device_id={"cols": lax.rem(me + 1, N_COLS)}, device_id_type=MESH,
    )

    xr[me] = xs[me]
    horizontal_weights(dk_ref, pw_ref, dk_pad, hw)
    vertical_weights(vw_ref, vw_pad, vw)
    bias_h = lane_tile(pb_ref[...], LANES)
    bias_v = lane_tile(vb_ref[...], LANES)
    edge = jnp.zeros((4, MSG, LANES), BF)
    for buffer in (recv, mid):
        buffer[0:4] = edge
        buffer[4 + Z : 8 + Z] = edge

    row = iota((TILES, LANES), 0)

    def horizontal(slot):
        y = odd * slot + (1 - odd) * (3 - slot)
        rows = jnp.concatenate([band[y + i] for i in range(KH)], axis=1)
        parts = dot(rows, hw[...])
        right = pltpu.roll(parts[:, 0:LANES], TILES - 1, 0)
        left = pltpu.roll(parts[:, 2 * LANES : 3 * LANES], 1, 0)
        total = (
            parts[:, LANES : 2 * LANES]
            + jnp.where(row < TILES - 1, right, 0.0)
            + jnp.where(row > 0, left, 0.0)
        )
        mixed = band[3 + y].astype(F32) + jax.nn.gelu(total + bias_h)
        send[:, slot * TILE : (slot + 1) * TILE, :] = mixed.astype(BF).reshape(N_COLS, TILE, LANES)

    late = lax.rem(me, N_Z) >= LATE

    @pl.when(late)
    def _():
        await_go()
        send_exhaust()

    near_arrival.wait_recv()
    first = 0
    for slot in range(YB):
        if slot > 0:

            @pl.when(has_far)
            def _():
                far_arrival(slot).wait_recv()

        horizontal(slot)
        if slot + 1 == GROUPS[0]:

            @pl.when(jnp.logical_not(late))
            def _():
                await_go()
                send_exhaust()

        if slot + 1 in GROUPS:
            part = slice(first * TILE, (slot + 1) * TILE)
            first = slot + 1

            @pl.loop(1, N_COLS)
            def _(s):
                there = lax.rem(me + s, N_COLS)
                pltpu.make_async_remote_copy(
                    src_ref=send.at[there, part], dst_ref=recv.at[4 + me, part],
                    send_sem=mix_send, recv_sem=mix_recv, device_id={"cols": there},
                    device_id_type=MESH,
                ).start()

    recv[4 + me] = send[me]
    all_exhaust.wait_recv()
    add_exhaust(xr, codes, rows_b, source)
    all_mixed.wait_recv()

    def conv(buffer, layer, block):
        levels = buffer[pl.ds(block * 2 * PAIRS, 2 * PAIRS + 8)].reshape(PAIRS + 4, 2, MSG, LANES)
        rows = jnp.concatenate(
            [levels[k // 2 : k // 2 + PAIRS, k % 2].reshape(PAIRS * MSG, LANES) for k in range(KV + 1)],
            axis=1,
        )
        wide = dot(rows, vw[layer])
        result = [
            levels[2 : 2 + PAIRS, j].astype(F32)
            + jax.nn.gelu(
                wide[:, j * LANES : (j + 1) * LANES] + bias_v[layer : layer + 1]
            ).reshape(PAIRS, MSG, LANES)
            for j in range(2)
        ]
        return jnp.stack(result, axis=1).reshape(2 * PAIRS, MSG, LANES)

    blocks = Z // (2 * PAIRS)
    size = 2 * PAIRS * MSG

    @pl.loop(0, blocks)
    def _(block):
        mid[pl.ds(block * 2 * PAIRS + 4, 2 * PAIRS)] = conv(recv, 0, block).astype(BF)

    @pl.loop(0, blocks)
    def _(block):
        base = pl.multiple_of(block * size, size)
        result = conv(mid, 1, block).reshape(size, LANES) + source[pl.ds(base, size), :]
        for level in range(2 * PAIRS):
            for slot in range(YB):
                y = odd * slot + (1 - odd) * (3 - slot)
                start = level * MSG + slot * TILE
                stage[pl.ds(base + level * MSG + y, TILE, stride=YB), :] = result[
                    start : start + TILE
                ]
        out_ref[pl.ds(base, size), :] = stage[pl.ds(base, size), :].astype(BF)

    near_copy.wait_send()

    @pl.when(has_far)
    def _():
        for j in range(1, 4):
            far_copy(j).wait_send()

    all_exhaust.wait_send()
    all_mixed.wait_send()


def body(
    field, depth_kernel, point_weight, point_bias, vert_weight, vert_bias, exhaust, owner, cells
):
    rows = field.reshape(YB, TILES, LANES).transpose(1, 0, 2).reshape(TILES * YB, LANES)
    out = pl.pallas_call(
        kernel,
        out_shape=jax.ShapeDtypeStruct((Z * MSG, LANES), BF),
        in_specs=[pl.BlockSpec(memory_space=pltpu.HBM)] * 9,
        out_specs=pl.BlockSpec(memory_space=pltpu.VMEM),
        scratch_shapes=[
            pltpu.VMEM((TILES * YB, LANES), BF),
            pltpu.VMEM((KH, KH, C), F32),
            pltpu.VMEM((C, C), BF),
            pltpu.VMEM((1, C), F32),
            pltpu.VMEM((LAYERS, C, KV * C), BF),
            pltpu.VMEM((LAYERS, C), F32),
            pltpu.VMEM((C, E_DEV), BF),
            pltpu.VMEM((1, E_DEV), jnp.int32),
            pltpu.VMEM((1, E_DEV), jnp.int32),
            pltpu.VMEM((TILES * YB, LANES), F32),
            pltpu.VMEM((YB + 6, TILES, LANES), BF),
            pltpu.VMEM((LANES, LANES), F32),
            pltpu.VMEM((KH * LANES, 3 * LANES), BF),
            pltpu.VMEM((LANES, 3 * LANES), F32),
            pltpu.VMEM((LAYERS, (KV + 1) * LANES, 2 * LANES), BF),
            pltpu.VMEM((N_COLS, MSG, LANES), BF),
            pltpu.VMEM((Z + 8, MSG, LANES), BF),
            pltpu.VMEM((Z + 8, MSG, LANES), BF),
            pltpu.VMEM((N_COLS, 16, LANES), BF),
            pltpu.VMEM((N_COLS, 16, LANES), BF),
            pltpu.VMEM((1, N_COLS * 32), F32),
            pltpu.VMEM((N_COLS * 32, LANES), BF),
            pltpu.VMEM((Z * MSG, LANES), F32),
            pltpu.SemaphoreType.DMA,
            pltpu.SemaphoreType.DMA,
            pltpu.SemaphoreType.DMA((3,)),
            pltpu.SemaphoreType.DMA((3,)),
            pltpu.SemaphoreType.DMA,
            pltpu.SemaphoreType.DMA,
            pltpu.SemaphoreType.DMA,
            pltpu.SemaphoreType.DMA,
            pltpu.SemaphoreType.REGULAR,
            pltpu.SemaphoreType.DMA((9,)),
        ],
        compiler_params=pltpu.CompilerParams(
            collective_id=0, has_side_effects=True, vmem_limit_bytes=48 * 1024 * 1024
        ),
    )(
        *(
            pltpu.with_memory_space_constraint(a, pltpu.HBM)
            for a in (
        rows, depth_kernel, point_weight, point_bias.reshape(1, C),
        vert_weight.transpose(0, 2, 1), vert_bias, exhaust.T, owner.reshape(1, E_DEV), cells.reshape(1, E_DEV),
            )
        )
    )
    return out.reshape(Z, MSG // YB, YB, LANES).transpose(0, 2, 1, 3).reshape(Z, YB, X * C // N_COLS)


def solution(mesh):
    placed = (
        P("cols", "rows", None),
        P(),
        P(),
        P(),
        P(),
        P(),
        P(("rows", "cols"), None),
        P(("rows", "cols"), None),
        P(("rows", "cols")),
    )
    return jax.shard_map(
        body, mesh=mesh, in_specs=placed, out_specs=P(None, "rows", "cols"), check_vma=False
    )
```
